256 devices in a mesh: seq: 32 (over z, y_lo, core), tp: 8 (over x, y_hi).
Axes of the slice: x: 4, y: 4 (y_hi: 2, y_lo: 2; y = y_hi * 2 + y_lo), z: 8, core: 2. Of those that a mesh axis runs over, the one named last changes fastest.
Arguments:
- q_raw: bfloat16 [2048, 5120], P('seq', 'tp'), may hold values from -160 to 160
- k_raw: bfloat16 [2048, 5120], P('seq', 'tp'), may hold values from -160 to 160
- v_new: bfloat16 [2048, 5120], P('seq', 'tp'), may hold values from -8 to 8
- q_gain: float32 [5120], P('tp'), may hold values from 1.5 to 3
- k_gain: float32 [5120], P('tp'), may hold values from 1 to 2
- cache_keys: bfloat16 [512, 128, 5120], P('seq', None, 'tp'), may hold values from -10 to 10
- cache_values: bfloat16 [512, 128, 5120], P('seq', None, 'tp'), may hold values from -8 to 8
- page_table: int32 [2, 256], replicated, may hold values from 0 to 511, as said below
- cached_lengths: int32 [2], replicated, may hold values from 6553 to 32768, as said below
- req_group: int32 [8], replicated, may hold values from 0 to 1, as said below
Outputs:
- attended: bfloat16 [2048, 5120], P('seq', 'tp')
The draws below stay inside these ranges and needn't reach their ends.
Inputs may be any that keep to these rules, and one draw needn't show every extreme that they name: `page_table`: the 256 pages of group g lie on distinct slots s with (s // 8) % 2 == g; every slot holds one page. `cached_lengths`: one group's length is exactly 32768. `req_group`: exactly 4 requests belong to each group.
All inputs are finite; a program needn't handle non-finite values.
Results may differ from the reference program's by a relative error of at most 0.013.
Values may be sent and summed in bfloat16 or wider, within the bound.
No kernel may reach another device: no remote copies, remote signals or barrier semaphores. Data moves between devices by JAX's collectives and lax.ppermute only.
A program may use at most 128 MiB of HBM per device.

```python
import math
import jax
import jax.numpy as jnp
from jax import lax

HEADS = 40
HDIM = 128
D = 5120
GROUPS = 2
PAGE = 128
CACHE_PAGES = 256
NEWTOK = 256
TOKENS = 2048
REQ = 8
GP_DEV = 8


def scaled_rows(key, salt):
    first, second, third = jax.random.split(jax.random.fold_in(key, salt), 3)
    columns = 3.0 ** (jnp.arange(D, dtype=jnp.float32) / (D - 1))
    columns = columns * jax.random.uniform(third, (D,), minval=0.8, maxval=1.25)
    row_scale = 10.0 ** jax.random.uniform(second, (TOKENS, 1))
    base = jax.random.truncated_normal(first, -4.0, 4.0, (TOKENS, D))
    return base * row_scale * columns


def draw_q_raw(key, part):
    values = scaled_rows(key, 11)
    return values.astype(jnp.bfloat16)


def draw_k_raw(key, part):
    return scaled_rows(key, 12).astype(jnp.bfloat16)


def draw_cache_keys(key, part):
    slot_count = GROUPS * CACHE_PAGES
    first = jax.random.fold_in(jax.random.fold_in(key, 31), 0)
    base = jax.random.truncated_normal(first, -6.0, 6.0, (slot_count, PAGE, D))
    return base.astype(jnp.bfloat16)


def draw_page_table(key, part):
    subkeys = jax.random.split(jax.random.fold_in(key, 21), GROUPS)
    orders = jax.vmap(lambda sub: jax.random.permutation(sub, CACHE_PAGES))(subkeys).astype(jnp.int32)
    group_ids = jnp.arange(GROUPS, dtype=jnp.int32)[:, None]
    slots = orders // GP_DEV * (GROUPS * GP_DEV) + group_ids * GP_DEV + orders % GP_DEV
    return slots.astype(jnp.int32)


def draw_cached_lengths(key, part):
    first, second = jax.random.split(jax.random.fold_in(key, 51))
    capacity = CACHE_PAGES * PAGE
    shorter = jax.random.randint(first, (GROUPS,), capacity // 5, 2 * capacity // 5 + 1)
    longest = jax.random.randint(second, (), 0, GROUPS)
    lengths = jnp.where(jnp.arange(GROUPS) == longest, capacity, shorter)
    return lengths.astype(jnp.int32)


def draw_req_group(key, part):
    order = jax.random.permutation(jax.random.fold_in(key, 41), REQ)
    return (order % GROUPS).astype(jnp.int32)


def level_of(rng, extent, cuts, smallest, high):
    def one(position, blocks):
        heights = jax.random.uniform(jax.random.fold_in(jax.random.fold_in(rng, 6), position), (blocks,), jnp.float32, smallest / len(cuts), high / len(cuts))
        return jnp.repeat(jnp.exp(heights), extent[position] // blocks).reshape((-1,) + (1,) * (len(extent) - position - 1))

    loudness = one(*cuts[0])
    for cut in cuts[1:]:
        loudness = loudness * one(*cut)
    return loudness


def normal_values(stream_key, dims, spread, most, shards=(), kind=jnp.bfloat16):
    drawn = spread * jax.random.normal(stream_key, dims, jnp.float32)
    if shards:
        drawn = drawn * level_of(stream_key, dims, shards, -0.22, 0.18)
    return jnp.clip(drawn, -most, most).astype(kind)


def setup_inputs(seed: int = 0) -> dict:
    key_list = jax.random.split(jax.random.key(seed), 11)
    q_raw = draw_q_raw(jax.random.fold_in(key_list[10], 71), 0)
    k_raw = draw_k_raw(jax.random.fold_in(key_list[10], 71), 0)
    v_new = normal_values(key_list[2], (TOKENS, D), 2.0, 8.0, ((0, 32), (1, 8)))
    q_gain = jnp.clip(1.5 + 1.5 * jax.random.uniform(key_list[3], (D,), jnp.float32) ** level_of(key_list[3], (D,), ((0, 8),), -0.2, 0.2), 1.5, 3.0)
    k_gain = jnp.clip(1.0 + 1.0 * jax.random.uniform(key_list[4], (D,), jnp.float32) ** level_of(key_list[4], (D,), ((0, 8),), -0.2, 0.2), 1.0, 2.0)
    cache_keys = draw_cache_keys(jax.random.fold_in(key_list[10], 71), 0)
    cache_values = normal_values(key_list[6], (GROUPS * CACHE_PAGES, PAGE, D), 2.0, 8.0, ((0, 32), (2, 8)))
    page_table = draw_page_table(jax.random.fold_in(key_list[10], 71), 0)
    cached_lengths = draw_cached_lengths(jax.random.fold_in(key_list[10], 71), 0)
    req_group = draw_req_group(jax.random.fold_in(key_list[10], 71), 0)
    return {"q_raw": q_raw, "k_raw": k_raw, "v_new": v_new, "q_gain": q_gain, "k_gain": k_gain, "cache_keys": cache_keys, "cache_values": cache_values, "page_table": page_table, "cached_lengths": cached_lengths, "req_group": req_group}


EPSILON = 1e-06
MASKED = -1e+30

def normalize(raw_rows, gain_row):
    values = raw_rows.astype(jnp.float32)
    mean_square = lax.optimization_barrier(jnp.mean(values * values, axis=-1, keepdims=True))
    return (values * lax.rsqrt(mean_square + EPSILON) * gain_row.astype(jnp.float32)[None, :]).astype(jnp.bfloat16)

def reference(q_raw, k_raw, v_new, q_gain, k_gain, cache_keys, cache_values, page_table, cached_lengths, req_group):
    requests = TOKENS // NEWTOK
    capacity = CACHE_PAGES * PAGE
    queries = normalize(q_raw, q_gain).reshape(requests, NEWTOK, HEADS, HDIM)
    new_keys = normalize(k_raw, k_gain).reshape(requests, NEWTOK, HEADS, HDIM)
    new_values = v_new.reshape(requests, NEWTOK, HEADS, HDIM)
    flat_table = page_table.reshape(-1).astype(jnp.int32)
    group_keys = cache_keys[flat_table].reshape(GROUPS, capacity, HEADS, HDIM)
    group_values = cache_values[flat_table].reshape(GROUPS, capacity, HEADS, HDIM)
    positions = jnp.arange(capacity, dtype=jnp.int32)
    factor = 1.0 / math.sqrt(HDIM)

    def one_request(request):
        group_id = req_group[request]
        usable = positions < cached_lengths[group_id]
        query_block = queries[request].astype(jnp.float32)
        cached_scores = jnp.einsum('qhd,khd->hqk', query_block, group_keys[group_id].astype(jnp.float32)) * factor
        own_scores = jnp.einsum('qhd,khd->hqk', query_block, new_keys[request].astype(jnp.float32)) * factor
        cached_scores = jnp.where(usable[None, None, :], cached_scores, MASKED)
        row_top = jnp.maximum(lax.optimization_barrier(jnp.max(cached_scores, axis=2)), lax.optimization_barrier(jnp.max(own_scores, axis=2)))
        cached_weights = jnp.where(usable[None, None, :], jnp.exp(cached_scores - row_top[:, :, None]), 0.0)
        own_weights = jnp.exp(own_scores - row_top[:, :, None])
        totals = lax.optimization_barrier(jnp.sum(cached_weights, axis=2)) + lax.optimization_barrier(jnp.sum(own_weights, axis=2))
        cached_round = lax.optimization_barrier(cached_weights.astype(jnp.bfloat16)).astype(jnp.float32)
        own_round = lax.optimization_barrier(own_weights.astype(jnp.bfloat16)).astype(jnp.float32)
        numerator = jnp.einsum('hqk,khd->qhd', cached_round, group_values[group_id].astype(jnp.float32))
        numerator = numerator + jnp.einsum('hqk,khd->qhd', own_round, new_values[request].astype(jnp.float32))
        result = numerator / jnp.transpose(totals)[:, :, None]
        return result.astype(jnp.bfloat16).reshape(NEWTOK, HEADS * HDIM)
    attended = lax.map(one_request, jnp.arange(requests, dtype=jnp.int32))
    return attended.reshape(TOKENS, HEADS * HDIM)
```

```python
import functools
import math

import jax
import jax.numpy as jnp
from jax import lax
from jax.experimental import pallas as pl
from jax.experimental.pallas import tpu as pltpu
from jax.sharding import PartitionSpec as P

HDIM = 128
GROUPS = 2
NEWTOK = 256
EPSILON = 1e-06
MASKED = -1e30
STAT_ROWS = 8


def pieces(values):
    high = values.astype(jnp.bfloat16)
    rest = values - high.astype(jnp.float32)
    middle = rest.astype(jnp.bfloat16)
    low = (rest - middle.astype(jnp.float32)).astype(jnp.bfloat16)
    return high, middle, low


def to_columns(rows):
    count = rows.shape[0]
    if count < 128:
        rows = jnp.concatenate([rows, jnp.zeros((128 - count, 128), jnp.float32)], axis=0)
    return rows.T


def sums_kernel(q_ref, k_ref, out_ref):
    tokens = q_ref.shape[0]
    query = q_ref[...].astype(jnp.float32)
    key = k_ref[...].astype(jnp.float32)
    query_sum = jnp.sum(query * query, axis=1, keepdims=True)
    key_sum = jnp.sum(key * key, axis=1, keepdims=True)
    lane = lax.broadcasted_iota(jnp.int32, (tokens, 128), 1)
    both = jnp.where(lane == 0, query_sum, jnp.where(lane == 1, key_sum, 0.0))
    padded = jnp.concatenate([both, jnp.zeros((128 - tokens, 128), jnp.float32)], axis=0)
    rows = padded.T[0:8]
    for index in range(out_ref.shape[0]):
        out_ref[index] = rows


def norm_kernel(q_ref, k_ref, v_ref, qg_ref, kg_ref, sums_ref, q_out, k_out, v_out, *, full_width, scale):
    tokens, width = q_ref.shape
    total = sums_ref[0]
    for index in range(1, sums_ref.shape[0]):
        total = total + sums_ref[index]
    inverse = to_columns(lax.rsqrt(total / full_width + EPSILON))
    query_inverse = inverse[0:tokens, 0:1]
    key_inverse = inverse[0:tokens, 1:2]
    q_out[...] = (
        q_ref[...].astype(jnp.float32) * query_inverse * (qg_ref[...] * scale)
    ).astype(jnp.bfloat16)
    k_out[0:tokens] = (
        k_ref[...].astype(jnp.float32) * key_inverse * kg_ref[...]
    ).astype(jnp.bfloat16)
    v_out[0:tokens] = v_ref[...]
    blank = jnp.zeros((k_out.shape[0] - tokens, width), jnp.bfloat16)
    k_out[tokens:] = blank
    v_out[tokens:] = blank


def attend_kernel(
    group_ref,
    length_ref,
    place_ref,
    table_ref,
    qa_ref,
    qb_ref,
    key_ref,
    value_ref,
    own_key_ref,
    own_value_ref,
    oa_ref,
    ob_ref,
    bias_ref,
    *,
    heads,
    pages,
    page_len,
    tok_dev,
):
    request = pl.program_id(0)
    group = group_ref[request]
    seq_index = place_ref[0]
    own_request = place_ref[1]
    cached = pages * page_len
    own_rows = own_key_ref.shape[0]

    @pl.when(request == 0)
    def _():
        lane = lax.broadcasted_iota(jnp.int32, (1, page_len), 1)
        page_ids = lax.broadcasted_iota(jnp.int32, (1, table_ref.shape[1]), 1)
        for group_id in range(GROUPS):
            table_row = table_ref[group_id : group_id + 1, :]
            for page in range(pages):
                slot = seq_index * (GROUPS * pages) + group_id * pages + page
                logical = jnp.sum(
                    jnp.where(table_row == slot, page_ids, 0), axis=1, keepdims=True
                )
                usable = logical * page_len + lane < length_ref[group_id]
                bias_ref[group_id, 0:1, page * page_len : (page + 1) * page_len] = jnp.where(
                    usable, 0.0, MASKED
                )

    def body(masked):
        if masked:
            own_lane = lax.broadcasted_iota(jnp.int32, (1, own_rows), 1)
            limit = jnp.where(request == own_request, tok_dev, 0)
            own_bias = jnp.where(own_lane < limit, 0.0, MASKED)
        for q_ref, o_ref in ((qa_ref, oa_ref), (qb_ref, ob_ref)):
            rows = q_ref.shape[1]
            lane = lax.broadcasted_iota(jnp.int32, (rows, 128), 1)
            stats = jnp.zeros((rows, 128), jnp.float32)
            for head in range(heads):
                columns = slice(head * HDIM, (head + 1) * HDIM)
                query = q_ref[0, :, columns]
                keys = key_ref[pl.ds(group * pages, pages), :, columns].reshape(cached, HDIM)
                values = value_ref[pl.ds(group * pages, pages), :, columns].reshape(cached, HDIM)
                scores = lax.dot_general(
                    query, keys, (((1,), (1,)), ((), ())), preferred_element_type=jnp.float32
                )
                if masked:
                    scores = scores + bias_ref[group]
                    own_scores = lax.dot_general(
                        query,
                        own_key_ref[:, columns],
                        (((1,), (1,)), ((), ())),
                        preferred_element_type=jnp.float32,
                    )
                    own_scores = own_scores + own_bias
                top = jnp.max(scores, axis=1, keepdims=True)
                if masked:
                    top = jnp.maximum(top, jnp.max(own_scores, axis=1, keepdims=True))
                weights = jnp.exp2(scores - top)
                total = jnp.sum(weights, axis=1, keepdims=True)
                mixed = jnp.dot(
                    weights.astype(jnp.bfloat16), values, preferred_element_type=jnp.float32
                )
                if masked:
                    own_weights = jnp.exp2(own_scores - top)
                    total = total + jnp.sum(own_weights, axis=1, keepdims=True)
                    mixed = mixed + jnp.dot(
                        own_weights.astype(jnp.bfloat16),
                        own_value_ref[:, columns],
                        preferred_element_type=jnp.float32,
                    )
                o_ref[0, 0:rows, columns] = (mixed * (1.0 / total)).astype(jnp.bfloat16)
                stats = jnp.where(lane == head, top + jnp.log2(total), stats)
            write_stats(o_ref, stats.T[0:STAT_ROWS], rows)

    plain = (length_ref[group] == table_ref.shape[1] * page_len) & (request != own_request)

    @pl.when(plain)
    def _():
        body(False)

    @pl.when(jnp.logical_not(plain))
    def _():
        body(True)


def write_stats(o_ref, stats, rows):
    for index, piece in enumerate(pieces(stats)):
        o_ref[0, rows : rows + STAT_ROWS, index * 128 : (index + 1) * 128] = piece
    left = o_ref.shape[2] - 3 * 128
    o_ref[0, rows : rows + STAT_ROWS, 3 * 128 :] = jnp.zeros((STAT_ROWS, left), jnp.bfloat16)


def read_stats(block, rows):
    stats = block[rows : rows + STAT_ROWS, 0:384].astype(jnp.float32)
    return stats[:, 0:128] + stats[:, 128:256] + stats[:, 256:384]


def pair_kernel(a_ref, b_ref, out_ref, *, heads):
    rows = a_ref.shape[1] - STAT_ROWS
    stat_a = read_stats(a_ref.at[0], rows)
    stat_b = read_stats(b_ref.at[0], rows)
    top = jnp.maximum(stat_a, stat_b)
    weight_a = jnp.exp2(stat_a - top)
    weight_b = jnp.exp2(stat_b - top)
    total = weight_a + weight_b
    factors = to_columns(jnp.concatenate([weight_a / total, weight_b / total], axis=0))
    for head in range(heads):
        columns = slice(head * HDIM, (head + 1) * HDIM)
        out_ref[0, 0:rows, columns] = (
            a_ref[0, 0:rows, columns].astype(jnp.float32) * factors[:, head : head + 1]
            + b_ref[0, 0:rows, columns].astype(jnp.float32)
            * factors[:, STAT_ROWS + head : STAT_ROWS + head + 1]
        ).astype(jnp.bfloat16)
    write_stats(out_ref, top + jnp.log2(total), rows)


def many_kernel(in_ref, keep_ref, send_ref, *, heads):
    count = in_ref.shape[0]
    rows = in_ref.shape[1] - STAT_ROWS
    half = rows // 2
    stats = [read_stats(in_ref.at[index], rows) for index in range(count)]
    top = functools.reduce(jnp.maximum, stats)
    weights = [jnp.exp2(stat - top) for stat in stats]
    total = functools.reduce(jnp.add, weights)
    factors = to_columns(jnp.concatenate([weight / total for weight in weights], axis=0))
    for head in range(heads):
        columns = slice(head * HDIM, (head + 1) * HDIM)
        merged = None
        for index in range(count):
            lane = index * STAT_ROWS + head
            term = in_ref[index, 0:rows, columns].astype(jnp.float32) * factors[:, lane : lane + 1]
            merged = term if merged is None else merged + term
        merged = merged.astype(jnp.bfloat16)
        keep_ref[0, 0:half, columns] = merged[0:half]
        send_ref[0, 0:half, columns] = merged[half:]
    stat = top + jnp.log2(total)
    write_stats(keep_ref, stat, half)
    swapped = jnp.concatenate([stat[:, half:], stat[:, 0:half]], axis=1)
    write_stats(send_ref, swapped, half)


def last_kernel(a_ref, b_ref, out_ref, *, heads):
    rows = out_ref.shape[0]
    stat_a = read_stats(a_ref.at[0], rows)
    stat_b = read_stats(b_ref.at[0], rows)
    top = jnp.maximum(stat_a, stat_b)
    weight_a = jnp.exp2(stat_a - top)
    weight_b = jnp.exp2(stat_b - top)
    total = weight_a + weight_b
    factors = to_columns(jnp.concatenate([weight_a / total, weight_b / total], axis=0))[0:rows]
    for head in range(heads):
        columns = slice(head * HDIM, (head + 1) * HDIM)
        out_ref[:, columns] = (
            a_ref[0, 0:rows, columns].astype(jnp.float32) * factors[:, head : head + 1]
            + b_ref[0, 0:rows, columns].astype(jnp.float32)
            * factors[:, STAT_ROWS + head : STAT_ROWS + head + 1]
        ).astype(jnp.bfloat16)


def on_device(
    q_raw,
    k_raw,
    v_new,
    q_gain,
    k_gain,
    cache_keys,
    cache_values,
    page_table,
    cached_lengths,
    req_group,
):
    tok_dev, width = q_raw.shape
    tp_count = lax.axis_size("tp")
    seq_count = lax.axis_size("seq")
    heads = width // HDIM
    page_len = cache_keys.shape[1]
    pages = cache_keys.shape[0] // GROUPS
    requests = req_group.shape[0]
    plane = seq_count // requests
    seq_index = lax.axis_index("seq")
    bf16 = jnp.bfloat16
    f32 = jnp.float32
    scale = math.log2(math.e) / math.sqrt(HDIM)
    z_groups = [[z * plane + member for z in range(requests)] for member in range(plane)]
    core_pairs = [(index, index ^ 1) for index in range(seq_count)]
    y_pairs = [(index, index ^ 2) for index in range(seq_count)]

    sums = pl.pallas_call(
        sums_kernel, out_shape=jax.ShapeDtypeStruct((tp_count, 8, 128), f32), name="sums"
    )(q_raw, k_raw)
    sums = lax.all_to_all(sums, "tp", split_axis=0, concat_axis=0, tiled=True)
    queries, own_keys, own_values = pl.pallas_call(
        functools.partial(norm_kernel, full_width=float(width * tp_count), scale=scale),
        out_shape=(
            jax.ShapeDtypeStruct((tok_dev, width), bf16),
            jax.ShapeDtypeStruct((128, width), bf16),
            jax.ShapeDtypeStruct((128, width), bf16),
        ),
        name="norm",
    )(q_raw, k_raw, v_new, q_gain[None, :], k_gain[None, :], sums)

    other = lax.ppermute(queries, "seq", y_pairs)
    rows = 2 * tok_dev
    mine = jnp.concatenate([queries, other], axis=0)
    spread = jnp.broadcast_to(mine[None], (requests, rows, width))
    queries_a = lax.all_to_all(
        spread, "seq", split_axis=0, concat_axis=0, tiled=True, axis_index_groups=z_groups
    )
    queries_b = lax.ppermute(queries_a, "seq", core_pairs)

    chunk = rows + STAT_ROWS
    place = jnp.stack([seq_index, seq_index // plane]).astype(jnp.int32)
    block_q = pl.BlockSpec((1, rows, width), lambda r, *_: (r, 0, 0))
    block_o = pl.BlockSpec((1, chunk, width), lambda r, *_: (r, 0, 0))
    whole = lambda array: pl.BlockSpec(array.shape, lambda r, *_: (0,) * array.ndim)
    partial_shape = jax.ShapeDtypeStruct((requests, chunk, width), bf16)
    out_a, out_b = pl.pallas_call(
        functools.partial(
            attend_kernel, heads=heads, pages=pages, page_len=page_len, tok_dev=tok_dev
        ),
        out_shape=(partial_shape, partial_shape),
        grid_spec=pltpu.PrefetchScalarGridSpec(
            num_scalar_prefetch=3,
            grid=(requests,),
            in_specs=[
                whole(page_table),
                block_q,
                block_q,
                whole(cache_keys),
                whole(cache_values),
                whole(own_keys),
                whole(own_values),
            ],
            out_specs=(block_o, block_o),
            scratch_shapes=[pltpu.VMEM((GROUPS, 1, pages * page_len), f32)],
        ),
        name="attend",
    )(
        req_group,
        cached_lengths,
        place,
        page_table,
        queries_a,
        queries_b,
        cache_keys,
        cache_values,
        own_keys,
        own_values,
    )

    out_b = lax.ppermute(out_b, "seq", core_pairs)
    merged = pl.pallas_call(
        functools.partial(pair_kernel, heads=heads),
        out_shape=partial_shape,
        grid=(requests,),
        in_specs=[pl.BlockSpec((1, chunk, width), lambda r: (r, 0, 0))] * 2,
        out_specs=pl.BlockSpec((1, chunk, width), lambda r: (r, 0, 0)),
        name="pair",
    )(out_a, out_b)
    merged = lax.all_to_all(
        merged, "seq", split_axis=0, concat_axis=0, tiled=True, axis_index_groups=z_groups
    )
    small = jax.ShapeDtypeStruct((1, tok_dev + STAT_ROWS, width), bf16)
    keep, send = pl.pallas_call(
        functools.partial(many_kernel, heads=heads), out_shape=(small, small), name="many"
    )(merged)
    send = lax.ppermute(send, "seq", y_pairs)
    return pl.pallas_call(
        functools.partial(last_kernel, heads=heads),
        out_shape=jax.ShapeDtypeStruct((tok_dev, width), bf16),
        name="last",
    )(keep, send)


def solution(mesh):
    return jax.shard_map(
        on_device,
        mesh=mesh,
        in_specs=(
            P("seq", "tp"),
            P("seq", "tp"),
            P("seq", "tp"),
            P("tp"),
            P("tp"),
            P("seq", None, "tp"),
            P("seq", None, "tp"),
            P(),
            P(),
            P(),
        ),
        out_specs=P("seq", "tp"),
        check_vma=False,
    )
```

```python
import functools
import math

import jax
import jax.numpy as jnp
from jax import lax
from jax.experimental import pallas as pl
from jax.experimental.pallas import tpu as pltpu
from jax.sharding import PartitionSpec as P

HDIM = 128
GROUPS = 2
NEWTOK = 256
EPSILON = 1e-06
MASKED = -1e30
STAT_ROWS = 8
SPLITS = ((0, 2), (2, 2), (4, 1))


def pieces(values):
    high = values.astype(jnp.bfloat16)
    rest = values - high.astype(jnp.float32)
    middle = rest.astype(jnp.bfloat16)
    low = (rest - middle.astype(jnp.float32)).astype(jnp.bfloat16)
    return high, middle, low


def to_columns(rows):
    count = rows.shape[0]
    if count < 128:
        rows = jnp.concatenate([rows, jnp.zeros((128 - count, 128), jnp.float32)], axis=0)
    return rows.T


def sums_kernel(q_ref, k_ref, out_ref):
    tokens = q_ref.shape[0]
    query = q_ref[...].astype(jnp.float32)
    key = k_ref[...].astype(jnp.float32)
    query_sum = jnp.sum(query * query, axis=1, keepdims=True)
    key_sum = jnp.sum(key * key, axis=1, keepdims=True)
    lane = lax.broadcasted_iota(jnp.int32, (tokens, 128), 1)
    both = jnp.where(lane == 0, query_sum, jnp.where(lane == 1, key_sum, 0.0))
    padded = jnp.concatenate([both, jnp.zeros((128 - tokens, 128), jnp.float32)], axis=0)
    rows = padded.T[0:8]
    for index in range(out_ref.shape[0]):
        out_ref[index] = rows


def norm_kernel(
    q_ref, k_ref, v_ref, qg_ref, kg_ref, sums_ref, *outs, full_width, scale, splits
):
    tokens, width = q_ref.shape
    spread_refs, (k_out, v_out) = outs[: len(splits)], outs[len(splits) :]
    total = sums_ref[0]
    for index in range(1, sums_ref.shape[0]):
        total = total + sums_ref[index]
    inverse = to_columns(lax.rsqrt(total / full_width + EPSILON))
    query_inverse = inverse[0:tokens, 0:1]
    key_inverse = inverse[0:tokens, 1:2]
    queries = (
        q_ref[...].astype(jnp.float32) * query_inverse * (qg_ref[...] * scale)
    ).astype(jnp.bfloat16)
    for (first, count), spread_ref in zip(splits, spread_refs):
        part = queries[:, first * HDIM : (first + count) * HDIM]
        for index in range(spread_ref.shape[0]):
            spread_ref[index] = part
    k_out[0:tokens] = (
        k_ref[...].astype(jnp.float32) * key_inverse * kg_ref[...]
    ).astype(jnp.bfloat16)
    v_out[0:tokens] = v_ref[...]
    blank = jnp.zeros((k_out.shape[0] - tokens, width), jnp.bfloat16)
    k_out[tokens:] = blank
    v_out[tokens:] = blank


def read_lse(ref, index, rows):
    found = []
    for first in range(0, ref.shape[2], HDIM):
        block = ref[index, rows : rows + STAT_ROWS, first : first + HDIM].astype(jnp.float32)
        found.append(block[0:1] + block[1:2] + block[2:3])
    return jnp.concatenate(found, axis=0)


def write_lse(ref, index, rows, lse):
    row = lax.broadcasted_iota(jnp.int32, (STAT_ROWS, 128), 0)
    for head in range(lse.shape[0]):
        high, middle, low = (
            piece.astype(jnp.float32) for piece in pieces(lse[head : head + 1])
        )
        block = jnp.where(
            row == 0, high, jnp.where(row == 1, middle, jnp.where(row == 2, low, 0.0))
        )
        ref[index, rows : rows + STAT_ROWS, head * HDIM : (head + 1) * HDIM] = block.astype(
            jnp.bfloat16
        )


def attend_kernel(
    group_ref,
    length_ref,
    place_ref,
    table_ref,
    q00_ref,
    q01_ref,
    q10_ref,
    q11_ref,
    key_ref,
    value_ref,
    own_key_ref,
    own_value_ref,
    oa_ref,
    ob_ref,
    bias_ref,
    *,
    first,
    pages,
    page_len,
    tok_dev,
):
    request = pl.program_id(0)
    group = group_ref[request]
    seq_index = place_ref[0]
    own_request = place_ref[1]
    cached = pages * page_len
    own_rows = own_key_ref.shape[0]
    heads = oa_ref.shape[2] // HDIM
    rows = 2 * tok_dev

    @pl.when(request == 0)
    def _():
        lane = lax.broadcasted_iota(jnp.int32, (1, page_len), 1)
        page_ids = lax.broadcasted_iota(jnp.int32, (1, table_ref.shape[1]), 1)
        for group_id in range(GROUPS):
            table_row = table_ref[group_id : group_id + 1, :]
            for page in range(pages):
                slot = seq_index * (GROUPS * pages) + group_id * pages + page
                logical = jnp.sum(
                    jnp.where(table_row == slot, page_ids, 0), axis=1, keepdims=True
                )
                usable = logical * page_len + lane < length_ref[group_id]
                bias_ref[group_id, 0:1, page * page_len : (page + 1) * page_len] = jnp.where(
                    usable, 0.0, MASKED
                )

    def body(masked):
        if masked:
            own_lane = lax.broadcasted_iota(jnp.int32, (1, own_rows), 1)
            limit = jnp.where(request == own_request, tok_dev, 0)
            own_bias = jnp.where(own_lane < limit, 0.0, MASKED)
        lane = lax.broadcasted_iota(jnp.int32, (2 * rows, 128), 1)
        stats = jnp.zeros((2 * rows, 128), jnp.float32)
        for head in range(heads):
            here = slice(head * HDIM, (head + 1) * HDIM)
            there = slice((first + head) * HDIM, (first + head + 1) * HDIM)
            query = jnp.concatenate(
                [ref[0, :, here] for ref in (q00_ref, q01_ref, q10_ref, q11_ref)], axis=0
            )
            keys = key_ref[pl.ds(group * pages, pages), :, here].reshape(cached, HDIM)
            values = value_ref[pl.ds(group * pages, pages), :, here].reshape(cached, HDIM)
            scores = lax.dot_general(
                query, keys, (((1,), (1,)), ((), ())), preferred_element_type=jnp.float32
            )
            if masked:
                scores = scores + bias_ref[group]
                own_scores = lax.dot_general(
                    query,
                    own_key_ref[:, there],
                    (((1,), (1,)), ((), ())),
                    preferred_element_type=jnp.float32,
                )
                own_scores = own_scores + own_bias
            top = jnp.max(scores, axis=1, keepdims=True)
            if masked:
                top = jnp.maximum(top, jnp.max(own_scores, axis=1, keepdims=True))
            weights = jnp.exp2(scores - top)
            total = jnp.sum(weights, axis=1, keepdims=True)
            mixed = jnp.dot(
                weights.astype(jnp.bfloat16), values, preferred_element_type=jnp.float32
            )
            if masked:
                own_weights = jnp.exp2(own_scores - top)
                total = total + jnp.sum(own_weights, axis=1, keepdims=True)
                mixed = mixed + jnp.dot(
                    own_weights.astype(jnp.bfloat16),
                    own_value_ref[:, there],
                    preferred_element_type=jnp.float32,
                )
            mixed = (mixed * (1.0 / total)).astype(jnp.bfloat16)
            oa_ref[0, 0:rows, here] = mixed[0:rows]
            ob_ref[0, 0:rows, here] = mixed[rows:]
            stats = jnp.where(lane == head, top + jnp.log2(total), stats)
        write_lse(oa_ref, 0, rows, stats[0:rows].T[0:heads])
        write_lse(ob_ref, 0, rows, stats[rows:].T[0:heads])

    plain = (length_ref[group] == table_ref.shape[1] * page_len) & (request != own_request)

    @pl.when(plain)
    def _():
        body(False)

    @pl.when(jnp.logical_not(plain))
    def _():
        body(True)


def merge_weights(stats):
    top = functools.reduce(jnp.maximum, stats)
    weights = [jnp.exp2(stat - top) for stat in stats]
    total = functools.reduce(jnp.add, weights)
    return [weight / total for weight in weights], top + jnp.log2(total)


def pair_kernel(a_ref, b_ref, *out_refs):
    count = a_ref.shape[0]
    rows = a_ref.shape[1] - STAT_ROWS
    heads = a_ref.shape[2] // HDIM
    factors = []
    joint = []
    for index in range(count):
        weights, lse = merge_weights([read_lse(a_ref, index, rows), read_lse(b_ref, index, rows)])
        factors += weights
        joint.append(lse)
    columns = to_columns(jnp.concatenate(factors, axis=0))[0:rows]
    part = rows // len(out_refs)
    for index in range(count):
        for head in range(heads):
            lane = 2 * index * heads + head
            here = slice(head * HDIM, (head + 1) * HDIM)
            merged = (
                a_ref[index, 0:rows, here].astype(jnp.float32) * columns[:, lane : lane + 1]
                + b_ref[index, 0:rows, here].astype(jnp.float32)
                * columns[:, lane + heads : lane + heads + 1]
            ).astype(jnp.bfloat16)
            for place, out_ref in enumerate(out_refs):
                out_ref[index, 0:part, here] = merged[place * part : (place + 1) * part]
        for place, out_ref in enumerate(out_refs):
            lse = joint[index]
            if place:
                lse = jnp.concatenate([lse[:, part:], lse[:, 0:part]], axis=1)
            write_lse(out_ref, index, part, lse)


def final_kernel(in_ref, *refs):
    out_ref = refs[-1]
    done = 0
    for ref in refs[:-1]:
        out_ref[:, done : done + ref.shape[1]] = ref[...]
        done += ref.shape[1]
    count = in_ref.shape[0]
    rows = in_ref.shape[1] - STAT_ROWS
    heads = in_ref.shape[2] // HDIM
    weights, _ = merge_weights([read_lse(in_ref, index, rows) for index in range(count)])
    columns = to_columns(jnp.concatenate(weights, axis=0))[0:rows]
    for head in range(heads):
        here = slice(head * HDIM, (head + 1) * HDIM)
        merged = None
        for index in range(count):
            lane = index * heads + head
            term = in_ref[index, 0:rows, here].astype(jnp.float32) * columns[:, lane : lane + 1]
            merged = term if merged is None else merged + term
        out_ref[:, done + head * HDIM : done + (head + 1) * HDIM] = merged.astype(jnp.bfloat16)


def merge_pairs(one, two, parts, step, name):
    count, size, width = one.shape
    rows = (size - STAT_ROWS) // parts + STAT_ROWS
    shape = jax.ShapeDtypeStruct((count, rows, width), jnp.bfloat16)
    out = pl.pallas_call(
        pair_kernel,
        out_shape=(shape,) * parts,
        grid=(count // step,),
        in_specs=[pl.BlockSpec((step, size, width), lambda r: (r, 0, 0))] * 2,
        out_specs=(pl.BlockSpec((step, rows, width), lambda r: (r, 0, 0)),) * parts,
        name=name,
    )(one, two)
    return out


def on_device(
    q_raw,
    k_raw,
    v_new,
    q_gain,
    k_gain,
    cache_keys,
    cache_values,
    page_table,
    cached_lengths,
    req_group,
):
    tok_dev, width = q_raw.shape
    tp_count = lax.axis_size("tp")
    seq_count = lax.axis_size("seq")
    heads = width // HDIM
    page_len = cache_keys.shape[1]
    pages = cache_keys.shape[0] // GROUPS
    requests = req_group.shape[0]
    plane = seq_count // requests
    seq_index = lax.axis_index("seq")
    bf16 = jnp.bfloat16
    f32 = jnp.float32
    scale = math.log2(math.e) / math.sqrt(HDIM)
    z_groups = [[z * plane + member for z in range(requests)] for member in range(plane)]
    core_pairs = [(index, index ^ 1) for index in range(seq_count)]
    y_pairs = [(index, index ^ 2) for index in range(seq_count)]
    splits = SPLITS

    def z_exchange(array):
        return lax.all_to_all(
            array, "seq", split_axis=0, concat_axis=0, tiled=True, axis_index_groups=z_groups
        )

    sums = pl.pallas_call(
        sums_kernel, out_shape=jax.ShapeDtypeStruct((tp_count, 8, 128), f32), name="sums"
    )(q_raw, k_raw)
    sums = lax.all_to_all(sums, "tp", split_axis=0, concat_axis=0, tiled=True)
    *spread, own_keys, own_values = pl.pallas_call(
        functools.partial(
            norm_kernel, full_width=float(width * tp_count), scale=scale, splits=splits
        ),
        out_shape=tuple(
            jax.ShapeDtypeStruct((requests, tok_dev, count * HDIM), bf16) for _, count in splits
        )
        + (jax.ShapeDtypeStruct((128, width), bf16),) * 2,
        name="norm",
    )(q_raw, k_raw, v_new, q_gain[None, :], k_gain[None, :], sums)

    place = jnp.stack([seq_index, seq_index // plane]).astype(jnp.int32)
    rows = 2 * tok_dev
    chunk = rows + STAT_ROWS

    def attend(first, count, queries):
        part = count * HDIM
        block_q = pl.BlockSpec((1, tok_dev, part), lambda r, *_: (r, 0, 0))
        block_o = pl.BlockSpec((1, chunk, part), lambda r, *_: (r, 0, 0))
        block_kv = pl.BlockSpec(
            (pl.Element(GROUPS * pages), pl.Element(page_len), pl.Element(part)), lambda r, *_: (0, 0, first * HDIM)
        )
        whole = lambda array: pl.BlockSpec(array.shape, lambda r, *_: (0,) * array.ndim)
        shape = jax.ShapeDtypeStruct((requests, chunk, part), bf16)
        return pl.pallas_call(
            functools.partial(
                attend_kernel, first=first, pages=pages, page_len=page_len, tok_dev=tok_dev
            ),
            out_shape=(shape, shape),
            grid_spec=pltpu.PrefetchScalarGridSpec(
                num_scalar_prefetch=3,
                grid=(requests,),
                in_specs=[whole(page_table)]
                + [block_q] * 4
                + [block_kv, block_kv, whole(own_keys), whole(own_values)],
                out_specs=(block_o, block_o),
                scratch_shapes=[pltpu.VMEM((GROUPS, 1, pages * page_len), f32)],
            ),
            name="attend",
        )(
            req_group,
            cached_lengths,
            place,
            page_table,
            *queries,
            cache_keys,
            cache_values,
            own_keys,
            own_values,
        )

    finished = []
    for (first, count), array in zip(splits, spread):
        q00 = z_exchange(array)
        q01 = lax.ppermute(q00, "seq", y_pairs)
        q10 = lax.ppermute(q00, "seq", core_pairs)
        q11 = lax.ppermute(q01, "seq", core_pairs)
        out_a, out_b = attend(first, count, (q00, q01, q10, q11))
        out_b = lax.ppermute(out_b, "seq", core_pairs)
        keep, send = merge_pairs(out_a, out_b, 2, requests // 2, "cores")
        send = lax.ppermute(send, "seq", y_pairs)
        (merged,) = merge_pairs(keep, send, 1, requests // 2, "sides")
        merged = z_exchange(merged)
        last = first + count == heads
        finished.append(
            pl.pallas_call(
                final_kernel,
                out_shape=jax.ShapeDtypeStruct(
                    (tok_dev, width if last else count * HDIM), bf16
                ),
                name="final",
            )(merged, *(finished if last else ()))
        )
    return finished[-1]


def solution(mesh):
    return jax.shard_map(
        on_device,
        mesh=mesh,
        in_specs=(
            P("seq", "tp"),
            P("seq", "tp"),
            P("seq", "tp"),
            P("tp"),
            P("tp"),
            P("seq", None, "tp"),
            P("seq", None, "tp"),
            P(),
            P(),
            P(),
        ),
        out_specs=P("seq", "tp"),
        check_vma=False,
    )
```

```python
import functools
import math

import jax
import jax.numpy as jnp
from jax import lax
from jax.experimental import pallas as pl
from jax.experimental.pallas import tpu as pltpu
from jax.sharding import PartitionSpec as P

HDIM = 128
GROUPS = 2
NEWTOK = 256
EPSILON = 1e-06
MASKED = -1e30
STAT_ROWS = 8


def pieces(values):
    high = values.astype(jnp.bfloat16)
    rest = values - high.astype(jnp.float32)
    middle = rest.astype(jnp.bfloat16)
    low = (rest - middle.astype(jnp.float32)).astype(jnp.bfloat16)
    return high, middle, low


def to_columns(rows):
    count = rows.shape[0]
    if count < 128:
        rows = jnp.concatenate([rows, jnp.zeros((128 - count, 128), jnp.float32)], axis=0)
    return rows.T


def sums_kernel(q_ref, k_ref, out_ref):
    tokens = q_ref.shape[0]
    query = q_ref[...].astype(jnp.float32)
    key = k_ref[...].astype(jnp.float32)
    query_sum = jnp.sum(query * query, axis=1, keepdims=True)
    key_sum = jnp.sum(key * key, axis=1, keepdims=True)
    lane = lax.broadcasted_iota(jnp.int32, (tokens, 128), 1)
    both = jnp.where(lane == 0, query_sum, jnp.where(lane == 1, key_sum, 0.0))
    padded = jnp.concatenate([both, jnp.zeros((128 - tokens, 128), jnp.float32)], axis=0)
    rows = padded.T[0:8]
    for index in range(out_ref.shape[0]):
        out_ref[index] = rows


def norm_kernel(q_ref, k_ref, v_ref, qg_ref, kg_ref, sums_ref, q_out, kv_out, *, full_width, scale):
    tokens = q_ref.shape[0]
    total = sums_ref[0]
    for index in range(1, sums_ref.shape[0]):
        total = total + sums_ref[index]
    inverse = to_columns(lax.rsqrt(total / full_width + EPSILON))
    query_inverse = inverse[0:tokens, 0:1]
    key_inverse = inverse[0:tokens, 1:2]
    q_out[...] = (
        q_ref[...].astype(jnp.float32) * query_inverse * (qg_ref[...] * scale)
    ).astype(jnp.bfloat16)
    kv_out[0] = (
        k_ref[...].astype(jnp.float32) * key_inverse * kg_ref[...]
    ).astype(jnp.bfloat16)
    kv_out[1] = v_ref[...]


def bias_kernel(length_ref, place_ref, table_ref, bias_ref, *, pages, page_len):
    lane = lax.broadcasted_iota(jnp.int32, (1, page_len), 1)
    page_ids = lax.broadcasted_iota(jnp.int32, (1, table_ref.shape[1]), 1)
    for group in range(GROUPS):
        table_row = table_ref[group : group + 1, :]
        for core in range(2):
            for page in range(pages):
                slot = (place_ref[core] * GROUPS + group) * pages + page
                logical = jnp.sum(
                    jnp.where(table_row == slot, page_ids, 0), axis=1, keepdims=True
                )
                usable = logical * page_len + lane < length_ref[group]
                column = (core * pages + page) * page_len
                bias_ref[group, :, column : column + page_len] = jnp.where(usable, 0.0, MASKED)


def read_lse(ref, rows):
    found = []
    for first in range(0, ref.shape[1], HDIM):
        block = ref[rows : rows + STAT_ROWS, first : first + HDIM].astype(jnp.float32)
        found.append(block[0:1] + block[1:2] + block[2:3])
    return jnp.concatenate(found, axis=0)


def write_lse(ref, rows, lse):
    row = lax.broadcasted_iota(jnp.int32, (STAT_ROWS, 128), 0)
    for head in range(lse.shape[0]):
        high, middle, low = (
            piece.astype(jnp.float32) for piece in pieces(lse[head : head + 1])
        )
        block = jnp.where(
            row == 0, high, jnp.where(row == 1, middle, jnp.where(row == 2, low, 0.0))
        )
        ref[rows : rows + STAT_ROWS, head * HDIM : (head + 1) * HDIM] = block.astype(jnp.bfloat16)


def transposed_dot(left, right):
    return lax.dot_general(
        left, right, (((1,), (1,)), ((), ())), preferred_element_type=jnp.float32
    )


def attend_kernel(
    group_ref, length_ref, request_ref, bias_ref, *refs, count, own, pages, page_len, capacity
):
    query_refs, refs = refs[:count], refs[count:]
    cache_refs, refs = (refs[0:2], refs[2:4]), refs[4:]
    if own:
        own_refs, refs = refs[:2], refs[2:]
    out_refs, stats_ref = refs[:count], refs[count]
    head = pl.program_id(0)
    heads = out_refs[0].shape[1] // HDIM
    rows = query_refs[0].shape[0]
    cached = pages * page_len
    here = pl.ds(pl.multiple_of(head * HDIM, HDIM), HDIM)
    lane = lax.broadcasted_iota(jnp.int32, (rows, 128), 1)

    def run(index, group, masked):
        query = query_refs[index][...]
        scores = []
        for core, (key_ref, _) in enumerate(cache_refs):
            keys = key_ref[pl.ds(group * pages, pages)].reshape(cached, HDIM)
            part = transposed_dot(query, keys)
            if masked:
                part = part + bias_ref[group, :, core * cached : (core + 1) * cached]
            scores.append(part)
        values = [
            value_ref[pl.ds(group * pages, pages)].reshape(cached, HDIM)
            for _, value_ref in cache_refs
        ]
        if own:
            scores.append(
                transposed_dot(query, jnp.concatenate([ref[0] for ref in own_refs], axis=0))
            )
            values.append(jnp.concatenate([ref[1] for ref in own_refs], axis=0))
        top = functools.reduce(
            jnp.maximum, [jnp.max(part, axis=1, keepdims=True) for part in scores]
        )
        total = None
        mixed = None
        for part, value in zip(scores, values):
            weights = jnp.exp2(part - top)
            more = jnp.sum(weights, axis=1, keepdims=True)
            term = jnp.dot(weights.astype(jnp.bfloat16), value, preferred_element_type=jnp.float32)
            total = more if total is None else total + more
            mixed = term if mixed is None else mixed + term
        out_refs[index][0:rows, here] = (mixed * (1.0 / total)).astype(jnp.bfloat16)
        stats_ref[index] = jnp.where(lane == head, top + jnp.log2(total), stats_ref[index])

    for index in range(count):
        group = group_ref[request_ref[index]]
        if own:
            run(index, group, True)
        else:
            full = length_ref[group] == capacity
            pl.when(full)(functools.partial(run, index, group, False))
            pl.when(jnp.logical_not(full))(functools.partial(run, index, group, True))

    @pl.when(head == heads - 1)
    def _():
        for index in range(count):
            write_lse(out_refs[index], rows, stats_ref[index].T[0:heads])


def merge_weights(stats):
    top = functools.reduce(jnp.maximum, stats)
    weights = [jnp.exp2(stat - top) for stat in stats]
    total = functools.reduce(jnp.add, weights)
    return [weight / total for weight in weights], top + jnp.log2(total)


def weighted(refs, rows, weights, head):
    heads = refs[0].shape[1] // HDIM
    here = slice(head * HDIM, (head + 1) * HDIM)
    merged = None
    for index, ref in enumerate(refs):
        lane = index * heads + head
        term = ref[0:rows, here].astype(jnp.float32) * weights[0:rows, lane : lane + 1]
        merged = term if merged is None else merged + term
    return merged.astype(jnp.bfloat16)


def gather_kernel(*refs):
    in_refs, (keep_ref, send_ref) = refs[:-2], refs[-2:]
    rows = in_refs[0].shape[0] - STAT_ROWS
    half = rows // 2
    weights, lse = merge_weights([read_lse(ref, rows) for ref in in_refs])
    columns = to_columns(jnp.concatenate(weights, axis=0))
    for head in range(lse.shape[0]):
        here = slice(head * HDIM, (head + 1) * HDIM)
        merged = weighted(in_refs, rows, columns, head)
        keep_ref[0:half, here] = merged[0:half]
        send_ref[0:half, here] = merged[half:]
    write_lse(keep_ref, half, lse)
    write_lse(send_ref, half, jnp.concatenate([lse[:, half:], lse[:, 0:half]], axis=1))


def last_kernel(one_ref, two_ref, out_ref):
    rows = out_ref.shape[0]
    weights, lse = merge_weights([read_lse(ref, rows) for ref in (one_ref, two_ref)])
    columns = to_columns(jnp.concatenate(weights, axis=0))
    for head in range(lse.shape[0]):
        out_ref[:, head * HDIM : (head + 1) * HDIM] = weighted(
            (one_ref, two_ref), rows, columns, head
        )


def on_device(
    q_raw,
    k_raw,
    v_new,
    q_gain,
    k_gain,
    cache_keys,
    cache_values,
    page_table,
    cached_lengths,
    req_group,
):
    tok_dev, width = q_raw.shape
    tp_count = lax.axis_size("tp")
    seq_count = lax.axis_size("seq")
    heads = width // HDIM
    page_len = cache_keys.shape[1]
    pages = cache_keys.shape[0] // GROUPS
    requests = req_group.shape[0]
    plane = seq_count // requests
    seq_index = lax.axis_index("seq")
    z_index = seq_index // plane
    bf16 = jnp.bfloat16
    f32 = jnp.float32
    scale = math.log2(math.e) / math.sqrt(HDIM)
    rows = 2 * tok_dev
    chunk = rows + STAT_ROWS
    cached = 2 * pages * page_len

    def along_z(array, distance):
        pairs = [(index, (index + distance * plane) % seq_count) for index in range(seq_count)]
        return lax.ppermute(array, "seq", pairs)

    def across(array, bit):
        return lax.ppermute(array, "seq", [(index, index ^ bit) for index in range(seq_count)])

    sums = pl.pallas_call(
        sums_kernel, out_shape=jax.ShapeDtypeStruct((tp_count, 8, 128), f32), name="sums"
    )(q_raw, k_raw)
    sums = lax.all_to_all(sums, "tp", split_axis=0, concat_axis=0, tiled=True)
    other_keys = across(cache_keys, 1)
    other_values = across(cache_values, 1)
    queries, own_kv = pl.pallas_call(
        functools.partial(norm_kernel, full_width=float(width * tp_count), scale=scale),
        out_shape=(
            jax.ShapeDtypeStruct((tok_dev, width), bf16),
            jax.ShapeDtypeStruct((2, tok_dev, width), bf16),
        ),
        name="norm",
    )(q_raw, k_raw, v_new, q_gain[None, :], k_gain[None, :], sums)
    other_kv = across(own_kv, 1)
    mine = jnp.concatenate([queries, across(queries, 2)], axis=0)

    places = jnp.stack([seq_index, seq_index ^ 1]).astype(jnp.int32)
    smem = pl.BlockSpec(memory_space=pltpu.SMEM)
    bias = pl.pallas_call(
        functools.partial(bias_kernel, pages=pages, page_len=page_len),
        out_shape=jax.ShapeDtypeStruct((GROUPS, 1, cached), f32),
        in_specs=[smem, smem, pl.BlockSpec(memory_space=pltpu.VMEM)],
        name="bias",
    )(cached_lengths, places, page_table)

    def attend(arrays, offsets, own):
        count = len(arrays)
        ids = jnp.stack([(z_index + offset) % requests for offset in offsets]).astype(jnp.int32)
        whole = lambda shape: pl.BlockSpec(shape, lambda h, *_: (0,) * len(shape))
        cache_spec = pl.BlockSpec((GROUPS * pages, page_len, HDIM), lambda h, *_: (0, 0, h))
        own_spec = pl.BlockSpec((2, tok_dev, HDIM), lambda h, *_: (0, 0, h))
        return pl.pallas_call(
            functools.partial(
                attend_kernel,
                count=count,
                own=own,
                pages=pages,
                page_len=page_len,
                capacity=page_table.shape[1] * page_len,
            ),
            out_shape=(jax.ShapeDtypeStruct((chunk, width), bf16),) * count,
            grid_spec=pltpu.PrefetchScalarGridSpec(
                num_scalar_prefetch=3,
                grid=(heads,),
                in_specs=[whole((GROUPS, 1, cached))]
                + [pl.BlockSpec((rows, HDIM), lambda h, *_: (0, h))] * count
                + [cache_spec] * 4
                + ([own_spec] * 2 if own else []),
                out_specs=(whole((chunk, width)),) * count,
                scratch_shapes=[pltpu.VMEM((count, rows, 128), f32)],
            ),
            name="attend",
        )(
            req_group,
            cached_lengths,
            ids,
            bias,
            *arrays,
            cache_keys,
            cache_values,
            other_keys,
            other_values,
            *((own_kv, other_kv) if own else ()),
        )

    steps = requests // 2
    below = above = mine
    arrived = []
    for step in range(1, steps + 1):
        below = along_z(below, 1)
        if step < requests - step:
            above = along_z(above, -1)
            arrived.append(((below, above), (-step, step)))
        else:
            arrived.append(((below,), (-step,)))
    partials = list(attend((mine,), (0,), True))
    for arrays, offsets in arrived:
        for result, offset in zip(attend(arrays, offsets, False), offsets):
            partials.append(along_z(result, offset))
    small = jax.ShapeDtypeStruct((tok_dev + STAT_ROWS, width), bf16)
    keep, send = pl.pallas_call(gather_kernel, out_shape=(small, small), name="gather")(*partials)
    return pl.pallas_call(
        last_kernel, out_shape=jax.ShapeDtypeStruct((tok_dev, width), bf16), name="last"
    )(keep, across(send, 2))


def solution(mesh):
    return jax.shard_map(
        on_device,
        mesh=mesh,
        in_specs=(
            P("seq", "tp"),
            P("seq", "tp"),
            P("seq", "tp"),
            P("tp"),
            P("tp"),
            P("seq", None, "tp"),
            P("seq", None, "tp"),
            P(),
            P(),
            P(),
        ),
        out_specs=P("seq", "tp"),
        check_vma=False,
    )
```

```python
import functools
import math

import jax
import jax.numpy as jnp
from jax import lax
from jax.experimental import pallas as pl
from jax.experimental.pallas import tpu as pltpu
from jax.sharding import PartitionSpec as P

HDIM = 128
GROUPS = 2
NEWTOK = 256
EPSILON = 1e-06
MASKED = -1e30
STAT_ROWS = 8
SMALL = pltpu.CompilerParams(vmem_limit_bytes=8 * 1024 * 1024)


def pieces(values):
    high = values.astype(jnp.bfloat16)
    rest = values - high.astype(jnp.float32)
    middle = rest.astype(jnp.bfloat16)
    low = (rest - middle.astype(jnp.float32)).astype(jnp.bfloat16)
    return high, middle, low


def to_columns(rows):
    count = rows.shape[0]
    if count < 128:
        rows = jnp.concatenate([rows, jnp.zeros((128 - count, 128), jnp.float32)], axis=0)
    return rows.T


def sums_kernel(q_ref, k_ref, out_ref):
    tokens = q_ref.shape[0]
    query = q_ref[...].astype(jnp.float32)
    key = k_ref[...].astype(jnp.float32)
    query_sum = jnp.sum(query * query, axis=1, keepdims=True)
    key_sum = jnp.sum(key * key, axis=1, keepdims=True)
    lane = lax.broadcasted_iota(jnp.int32, (tokens, 128), 1)
    both = jnp.where(lane == 0, query_sum, jnp.where(lane == 1, key_sum, 0.0))
    padded = jnp.concatenate([both, jnp.zeros((128 - tokens, 128), jnp.float32)], axis=0)
    rows = padded.T[0:8]
    for index in range(out_ref.shape[0]):
        out_ref[index] = rows


def norm_kernel(q_ref, k_ref, v_ref, qg_ref, kg_ref, sums_ref, q_out, kv_out, *, full_width, scale):
    tokens = q_ref.shape[0]
    total = sums_ref[0]
    for index in range(1, sums_ref.shape[0]):
        total = total + sums_ref[index]
    inverse = to_columns(lax.rsqrt(total / full_width + EPSILON))
    query_inverse = inverse[0:tokens, 0:1]
    key_inverse = inverse[0:tokens, 1:2]
    q_out[...] = (
        q_ref[...].astype(jnp.float32) * query_inverse * (qg_ref[...] * scale)
    ).astype(jnp.bfloat16)
    kv_out[0] = (
        k_ref[...].astype(jnp.float32) * key_inverse * kg_ref[...]
    ).astype(jnp.bfloat16)
    kv_out[1] = v_ref[...]


def bias_kernel(length_ref, place_ref, table_ref, bias_ref, *, pages, page_len):
    lane = lax.broadcasted_iota(jnp.int32, (1, page_len), 1)
    page_ids = lax.broadcasted_iota(jnp.int32, (1, table_ref.shape[1]), 1)
    for group in range(GROUPS):
        table_row = table_ref[group : group + 1, :]
        for core in range(2):
            for page in range(pages):
                slot = (place_ref[core] * GROUPS + group) * pages + page
                logical = jnp.sum(
                    jnp.where(table_row == slot, page_ids, 0), axis=1, keepdims=True
                )
                usable = logical * page_len + lane < length_ref[group]
                column = (core * pages + page) * page_len
                bias_ref[group, :, column : column + page_len] = jnp.where(usable, 0.0, MASKED)


def read_lse(ref, rows):
    found = []
    for first in range(0, ref.shape[1], HDIM):
        block = ref[rows : rows + STAT_ROWS, first : first + HDIM].astype(jnp.float32)
        found.append(block[0:1] + block[1:2] + block[2:3])
    return jnp.concatenate(found, axis=0)


def write_lse(ref, rows, lse):
    row = lax.broadcasted_iota(jnp.int32, (STAT_ROWS, 128), 0)
    for head in range(lse.shape[0]):
        high, middle, low = (
            piece.astype(jnp.float32) for piece in pieces(lse[head : head + 1])
        )
        block = jnp.where(
            row == 0, high, jnp.where(row == 1, middle, jnp.where(row == 2, low, 0.0))
        )
        ref[rows : rows + STAT_ROWS, head * HDIM : (head + 1) * HDIM] = block.astype(jnp.bfloat16)


def transposed_dot(left, right):
    return lax.dot_general(
        left, right, (((1,), (1,)), ((), ())), preferred_element_type=jnp.float32
    )


def attend_kernel(
    group_ref, length_ref, place_ref, bias_ref, *refs, offsets, own, pages, page_len, capacity
):
    count = len(offsets)
    query_refs, refs = refs[:count], refs[count:]
    cache_refs, refs = (refs[0:2], refs[2:4]), refs[4:]
    if own:
        own_refs, refs = refs[:2], refs[2:]
    out_refs, stats_ref = refs[:count], refs[count]
    head = pl.program_id(0)
    heads = out_refs[0].shape[1] // HDIM
    rows = query_refs[0].shape[0]
    cached = pages * page_len
    here = pl.ds(pl.multiple_of(head * HDIM, HDIM), HDIM)
    lane = lax.broadcasted_iota(jnp.int32, (rows, 128), 1)

    def run(index, group, masked):
        query = query_refs[index][...]
        scores = []
        for core, (key_ref, _) in enumerate(cache_refs):
            keys = key_ref[pl.ds(group * pages, pages), :, here].reshape(cached, HDIM)
            part = transposed_dot(query, keys)
            if masked:
                part = part + bias_ref[group, :, core * cached : (core + 1) * cached]
            scores.append(part)
        values = [
            value_ref[pl.ds(group * pages, pages), :, here].reshape(cached, HDIM)
            for _, value_ref in cache_refs
        ]
        if own:
            scores.append(
                transposed_dot(query, jnp.concatenate([ref[0] for ref in own_refs], axis=0))
            )
            values.append(jnp.concatenate([ref[1] for ref in own_refs], axis=0))
        top = functools.reduce(
            jnp.maximum, [jnp.max(part, axis=1, keepdims=True) for part in scores]
        )
        total = None
        mixed = None
        for part, value in zip(scores, values):
            weights = jnp.exp2(part - top)
            more = jnp.sum(weights, axis=1, keepdims=True)
            term = jnp.dot(weights.astype(jnp.bfloat16), value, preferred_element_type=jnp.float32)
            total = more if total is None else total + more
            mixed = term if mixed is None else mixed + term
        out_refs[index][0:rows, here] = (mixed * (1.0 / total)).astype(jnp.bfloat16)
        stats_ref[index] = jnp.where(lane == head, top + jnp.log2(total), stats_ref[index])

    for index in range(count):
        group = group_ref[lax.rem(place_ref[2] + offsets[index], group_ref.shape[0])]
        if own:
            run(index, group, True)
        else:
            full = length_ref[group] == capacity
            pl.when(full)(functools.partial(run, index, group, False))
            pl.when(jnp.logical_not(full))(functools.partial(run, index, group, True))

    @pl.when(head == heads - 1)
    def _():
        for index in range(count):
            write_lse(out_refs[index], rows, stats_ref[index].T[0:heads])


def merge_weights(stats):
    top = functools.reduce(jnp.maximum, stats)
    weights = [jnp.exp2(stat - top) for stat in stats]
    total = functools.reduce(jnp.add, weights)
    return [weight / total for weight in weights], top + jnp.log2(total)


def weighted(refs, rows, weights, head):
    heads = refs[0].shape[1] // HDIM
    here = slice(head * HDIM, (head + 1) * HDIM)
    merged = None
    for index, ref in enumerate(refs):
        lane = index * heads + head
        term = ref[0:rows, here].astype(jnp.float32) * weights[0:rows, lane : lane + 1]
        merged = term if merged is None else merged + term
    return merged.astype(jnp.bfloat16)


def gather_kernel(*refs):
    in_refs, (keep_ref, send_ref) = refs[:-2], refs[-2:]
    rows = in_refs[0].shape[0] - STAT_ROWS
    half = rows // 2
    weights, lse = merge_weights([read_lse(ref, rows) for ref in in_refs])
    columns = to_columns(jnp.concatenate(weights, axis=0))
    for head in range(lse.shape[0]):
        here = slice(head * HDIM, (head + 1) * HDIM)
        merged = weighted(in_refs, rows, columns, head)
        keep_ref[0:half, here] = merged[0:half]
        send_ref[0:half, here] = merged[half:]
    write_lse(keep_ref, half, lse)
    write_lse(send_ref, half, jnp.concatenate([lse[:, half:], lse[:, 0:half]], axis=1))


def last_kernel(one_ref, two_ref, out_ref):
    rows = out_ref.shape[0]
    weights, lse = merge_weights([read_lse(ref, rows) for ref in (one_ref, two_ref)])
    columns = to_columns(jnp.concatenate(weights, axis=0))
    for head in range(lse.shape[0]):
        out_ref[:, head * HDIM : (head + 1) * HDIM] = weighted(
            (one_ref, two_ref), rows, columns, head
        )


def on_device(
    q_raw,
    k_raw,
    v_new,
    q_gain,
    k_gain,
    cache_keys,
    cache_values,
    page_table,
    cached_lengths,
    req_group,
):
    tok_dev, width = q_raw.shape
    tp_count = lax.axis_size("tp")
    seq_count = lax.axis_size("seq")
    heads = width // HDIM
    page_len = cache_keys.shape[1]
    pages = cache_keys.shape[0] // GROUPS
    requests = req_group.shape[0]
    plane = seq_count // requests
    seq_index = lax.axis_index("seq")
    z_index = seq_index // plane
    bf16 = jnp.bfloat16
    f32 = jnp.float32
    scale = math.log2(math.e) / math.sqrt(HDIM)
    rows = 2 * tok_dev
    chunk = rows + STAT_ROWS
    cached = 2 * pages * page_len

    def along_z(array, distance):
        pairs = [(index, (index + distance * plane) % seq_count) for index in range(seq_count)]
        return lax.ppermute(array, "seq", pairs)

    def across(array, bit):
        return lax.ppermute(array, "seq", [(index, index ^ bit) for index in range(seq_count)])

    sums = pl.pallas_call(
        sums_kernel, out_shape=jax.ShapeDtypeStruct((tp_count, 8, 128), f32), compiler_params=SMALL, name="sums"
    )(q_raw, k_raw)
    sums = lax.all_to_all(sums, "tp", split_axis=0, concat_axis=0, tiled=True)
    other_keys = across(cache_keys, 1)
    other_values = across(cache_values, 1)
    queries, own_kv = pl.pallas_call(
        functools.partial(norm_kernel, full_width=float(width * tp_count), scale=scale),
        out_shape=(
            jax.ShapeDtypeStruct((tok_dev, width), bf16),
            jax.ShapeDtypeStruct((2, tok_dev, width), bf16),
        ),
        compiler_params=SMALL, name="norm",
    )(q_raw, k_raw, v_new, q_gain[None, :], k_gain[None, :], sums)
    other_kv = across(own_kv, 1)
    mine = jnp.concatenate([queries, across(queries, 2)], axis=0)

    places = jnp.stack([seq_index, seq_index ^ 1, z_index]).astype(jnp.int32)
    smem = pl.BlockSpec(memory_space=pltpu.SMEM)
    bias = pl.pallas_call(
        functools.partial(bias_kernel, pages=pages, page_len=page_len),
        out_shape=jax.ShapeDtypeStruct((GROUPS, 1, cached), f32),
        in_specs=[smem, smem, pl.BlockSpec(memory_space=pltpu.VMEM)],
        compiler_params=SMALL, name="bias",
    )(cached_lengths, places, page_table)

    caches = [
        pltpu.with_memory_space_constraint(array, pltpu.VMEM)
        for array in (cache_keys, cache_values, other_keys, other_values)
    ]

    def attend(arrays, offsets, own):
        count = len(arrays)
        whole = lambda shape: pl.BlockSpec(shape, lambda h, *_: (0,) * len(shape))
        cache_spec = pl.BlockSpec(memory_space=pltpu.VMEM)
        own_spec = pl.BlockSpec((2, tok_dev, HDIM), lambda h, *_: (0, 0, h))
        return pl.pallas_call(
            functools.partial(
                attend_kernel,
                offsets=tuple(offset % requests for offset in offsets),
                own=own,
                pages=pages,
                page_len=page_len,
                capacity=page_table.shape[1] * page_len,
            ),
            out_shape=(jax.ShapeDtypeStruct((chunk, width), bf16),) * count,
            grid_spec=pltpu.PrefetchScalarGridSpec(
                num_scalar_prefetch=3,
                grid=(heads,),
                in_specs=[whole((GROUPS, 1, cached))]
                + [pl.BlockSpec((rows, HDIM), lambda h, *_: (0, h))] * count
                + [cache_spec] * 4
                + ([own_spec] * 2 if own else []),
                out_specs=(whole((chunk, width)),) * count,
                scratch_shapes=[pltpu.VMEM((count, rows, 128), f32)],
            ),
            compiler_params=pltpu.CompilerParams(vmem_limit_bytes=20 * 1024 * 1024),
            name="attend",
        )(
            req_group,
            cached_lengths,
            places,
            bias,
            *arrays,
            *caches,
            *((own_kv, other_kv) if own else ()),
        )

    partials = []
    steps = requests // 2
    below = above = mine
    held, offsets, own = (mine,), (0,), True
    for step in range(1, steps + 1):
        both = step < requests - step
        below = along_z(below, 1)
        above = along_z(above, -1) if both else above
        results = attend(held, offsets, own)
        if step < steps:
            below, above, results = lax.optimization_barrier((below, above, results))
        partials += [
            along_z(result, offset) if offset else result
            for result, offset in zip(results, offsets)
        ]
        held = (below, above) if both else (below,)
        offsets, own = ((-step, step) if both else (-step,)), False
    results = attend(held, offsets, own)
    partials += [along_z(result, offset) for result, offset in zip(results, offsets)]
    small = jax.ShapeDtypeStruct((tok_dev + STAT_ROWS, width), bf16)
    keep, send = pl.pallas_call(gather_kernel, out_shape=(small, small), compiler_params=SMALL, name="gather")(*partials)
    return pl.pallas_call(
        last_kernel, out_shape=jax.ShapeDtypeStruct((tok_dev, width), bf16), compiler_params=SMALL, name="last"
    )(keep, across(send, 2))


def solution(mesh):
    return jax.shard_map(
        on_device,
        mesh=mesh,
        in_specs=(
            P("seq", "tp"),
            P("seq", "tp"),
            P("seq", "tp"),
            P("tp"),
            P("tp"),
            P("seq", None, "tp"),
            P("seq", None, "tp"),
            P(),
            P(),
            P(),
        ),
        out_specs=P("seq", "tp"),
        check_vma=False,
    )
```
